32 devices in a mesh: section: 2 (over core), dp: 4 (over z), tensor: 4 (over y, x).
Axes of the slice: x: 2, y: 2, z: 4, core: 2. Of those that a mesh axis runs over, the one named last changes fastest.
Arguments:
- boundary: bfloat16 [2, 4, 196, 24, 512], P('section', None, 'tensor', 'dp'), may hold values from -11 to 11
- live: int32 [4, 4], P(None, 'dp'), may hold values from 1 to 6, 18 in all within a row
- w_qkv: bfloat16 [2, 512, 3, 512], P('section', 'dp', None, 'tensor'), may hold values from -0.25 to 0.25
- w_proj: bfloat16 [2, 512, 512], P('section', 'tensor', 'dp'), may hold values from -1 to 1
- w_fc1: bfloat16 [2, 512, 2048], P('section', 'dp', 'tensor'), may hold values from -0.25 to 0.25
- w_fc2: bfloat16 [2, 2048, 512], P('section', 'tensor', 'dp'), may hold values from -0.125 to 0.125
- gains: bfloat16 [2, 2, 512], P('section', None, 'dp'), may hold values from 0.25 to 1.75
- biases: bfloat16 [2, 10, 512], P('section', None, 'dp'), may hold values from -3 to 3
Outputs:
- results: float32 [2, 4, 196, 24, 512], P('section', None, 'tensor', 'dp')
- grad_qkv: float32 [2, 512, 3, 512], P('section', 'dp', None, 'tensor')
- grad_proj: float32 [2, 512, 512], P('section', 'tensor', 'dp')
- grad_fc1: float32 [2, 512, 2048], P('section', 'dp', 'tensor')
- grad_fc2: float32 [2, 2048, 512], P('section', 'tensor', 'dp')
- grad_gains: float32 [2, 2, 512], P('section', None, ('dp', 'tensor'))
- grad_biases: float32 [2, 10, 512], P('section', None, ('dp', 'tensor'))
The draws below stay inside these ranges and needn't reach their ends.
Inputs may be any that keep to these rules, and one draw needn't show every extreme that they name: live[m, j] of the 6 slots of data-axis index j are used in micro-batch m, the first ones; each micro-batch uses 3 * 6 * 1 images, and in each some index uses all 6.
All inputs are finite; a program needn't handle non-finite values. No bound on the sum of `live` on one device may be relied on, other than what follows from the above.
Results may differ from the reference program's by a relative error of at most 0.033.
Values may be sent and summed in bfloat16 or wider, within the bound.
No kernel may reach another device: no remote copies, remote signals or barrier semaphores. Data moves between devices by JAX's collectives and lax.ppermute only.
A program may use at most 256 MiB of HBM per device.

```python
import math
import jax
import jax.numpy as jnp
import numpy as np
from jax import lax

D = 512
HEAD_DIM = 32
FF = 2048
GRID = 14
WIN = 7
SHIFT = 3
MICRO = 4
SLOTS = 6
TOK_IMG = 196
IMAGES = 24
NBIAS = 10
N_DP = 4
N_TENSOR = 4


def draw_boundary(key, part):
    keys = jax.random.split(key, 2)
    shape = (2, MICRO, TOK_IMG, IMAGES, D)
    column = jnp.exp(jax.random.uniform(keys[1], (D,), jnp.float32, jnp.log(0.3), jnp.log(3.0)))
    values = jax.random.truncated_normal(keys[0], -3.5, 3.5, shape, jnp.float32) * column
    return values.astype(jnp.bfloat16)


def steps_of(rng, shape, cuts, least, top_value):
    level, own = 1.0, jax.random.fold_in(rng, 6)
    for dim, blocks in cuts:
        steps = jnp.exp(jax.random.uniform(jax.random.fold_in(own, dim), (blocks,), jnp.float32, least / len(cuts), top_value / len(cuts)))
        level = level * jnp.repeat(steps, shape[dim] // blocks).reshape([-1 if axis == dim else 1 for axis in range(len(shape))])
    return level


def profile(count, total, limit, skew):
    portions = [(1 << 20) // math.isqrt(rank ** skew) + 1 for rank in range(2, count + 1)]
    rest, given = total - limit - (count - 1), [1] * (count - 1)
    while rest > 0:
        movable = [i for i in range(count - 1) if given[i] < limit]
        whole, budget = sum([portions[i] for i in movable]), rest
        for i in movable:
            more = min(limit - given[i], max(1, budget * portions[i] // whole), rest)
            given[i] = given[i] + more
            rest = rest - more
    return np.array([limit] + given)


def uneven_parts(rng, amount, total, reach, lean):
    if amount == 2:
        one = jax.random.randint(rng, (), max(1, total - reach), min(reach, total - 1) + 1)
        return jnp.stack([one, total - one])
    sizes = jnp.asarray(profile(amount, total, reach, lean), jnp.int32)
    couples = (amount - 1) // 2
    donor, taker = sizes[1:1 + 2 * couples:2], sizes[2:2 + 2 * couples:2]
    slack = jnp.minimum(donor - 1, reach - taker)
    moved = jax.random.randint(jax.random.fold_in(rng, 1), (couples,), 0, 1 << 20) % (slack + 1)
    sizes = sizes.at[1:1 + 2 * couples:2].set(donor - moved).at[2:2 + 2 * couples:2].set(taker + moved)
    return sizes[jax.random.permutation(jax.random.fold_in(rng, 2), amount)]


def normal_values(key, extent, deviation, most, pieces=(), dtype=jnp.bfloat16):
    loudness = steps_of(key, extent, pieces, -0.22, 0.18) if pieces else 1.0
    entries = jax.random.normal(key, extent, jnp.float32) * deviation * loudness
    return jnp.minimum(jnp.maximum(entries, -most), most).astype(dtype)


def setup_inputs(seed: int = 0) -> dict:
    streams_of = jax.random.split(jax.random.key(seed), 9)
    boundary = draw_boundary(jax.random.fold_in(streams_of[8], 71), 0)
    live = jax.vmap(lambda own: uneven_parts(own, N_DP, 3 * SLOTS * N_DP // 4, SLOTS, 1))(jax.random.split(streams_of[1], MICRO)).reshape((MICRO, N_DP)).astype(jnp.int32)
    w_qkv = normal_values(streams_of[2], (2, D, 3, D), D ** -0.5, 0.25, ((0, 2), (1, 4), (3, 4)))
    w_proj = normal_values(streams_of[3], (2, D, D), (D // 16) ** -0.5, 1.0, ((0, 2), (1, 4), (2, 4)))
    w_fc1 = normal_values(streams_of[4], (2, D, FF), D ** -0.5, 0.25, ((0, 2), (1, 4), (2, 4)))
    w_fc2 = normal_values(streams_of[5], (2, FF, D), FF ** -0.5, 0.125, ((0, 2), (1, 4), (2, 4)))
    gains = jnp.clip(1.0 + 0.15 * jax.random.normal(streams_of[6], (2, 2, D), jnp.float32), 0.25, 1.75).astype(jnp.bfloat16)
    biases = normal_values(streams_of[7], (2, NBIAS, D), 0.3, 3.0, ((0, 2), (2, 4)))
    return {"boundary": boundary, "live": live, "w_qkv": w_qkv, "w_proj": w_proj, "w_fc1": w_fc1, "w_fc2": w_fc2, "gains": gains, "biases": biases}


EPSILON = 1e-05

def layer_norm(values, gain, offset):
    centre = lax.optimization_barrier(jnp.mean(values, axis=-1, keepdims=True))
    centred = values - centre
    inverse = lax.rsqrt(lax.optimization_barrier(jnp.mean(centred * centred, axis=-1, keepdims=True)) + EPSILON)
    normal = centred * inverse
    return (normal * gain + offset, normal, inverse)

def norm_back(grad, normal, inverse, gain):
    scaled = grad * gain
    return inverse * (scaled - lax.optimization_barrier(jnp.mean(scaled, axis=-1, keepdims=True)) - normal * lax.optimization_barrier(jnp.mean(scaled * normal, axis=-1, keepdims=True)))

def exact_gelu(values):
    return jax.nn.gelu(values, approximate=False)

def round_trip(values):
    return lax.optimization_barrier(values.astype(jnp.bfloat16)).astype(jnp.float32)

def group_sum(term, groups):
    total = round_trip(term(0))
    for index in range(1, groups):
        total = total + round_trip(term(index))
    return total

def window_keep(shifted, images):
    per_side = GRID // WIN
    coord = jnp.arange(GRID)
    band = (coord >= GRID - WIN).astype(jnp.int32) + (coord >= GRID - SHIFT).astype(jnp.int32)
    region = (band[:, None] * 3 + band[None, :]).reshape(per_side, WIN, per_side, WIN)
    region = region.transpose(0, 2, 1, 3).reshape(per_side * per_side, WIN * WIN)
    allowed = (region[:, :, None] == region[:, None, :]).astype(jnp.float32)
    if not shifted:
        allowed = jnp.ones_like(allowed)
    allowed = jnp.broadcast_to(allowed[None], (images, per_side * per_side, WIN * WIN, WIN * WIN))
    return allowed.reshape(images * per_side * per_side, 1, WIN * WIN, WIN * WIN)

def to_windows(values, shifted):
    images, channels = (values.shape[1], values.shape[2])
    token_grid = values.reshape(GRID, GRID, images, channels)
    if shifted:
        token_grid = jnp.roll(token_grid, (-SHIFT, -SHIFT), (0, 1))
    per_side = GRID // WIN
    token_grid = token_grid.reshape(per_side, WIN, per_side, WIN, images, channels)
    return token_grid.transpose(4, 0, 2, 1, 3, 5).reshape(images * per_side * per_side, WIN * WIN, channels)

def from_windows(values, images, shifted):
    per_side = GRID // WIN
    channels = values.shape[-1]
    token_grid = values.reshape(images, per_side, per_side, WIN, WIN, channels)
    token_grid = token_grid.transpose(1, 3, 2, 4, 0, 5).reshape(GRID, GRID, images, channels)
    if shifted:
        token_grid = jnp.roll(token_grid, (SHIFT, SHIFT), (0, 1))
    return token_grid.reshape(GRID * GRID, images, channels)

def attend(windows, allowed):
    score_scale = HEAD_DIM ** (-0.5)
    query_rows = windows[:, :, 0].astype(jnp.float32)
    key_rows = windows[:, :, 1].astype(jnp.float32)
    value_rows = windows[:, :, 2].astype(jnp.float32)
    scores = jnp.einsum('wqhe,wkhe->whqk', query_rows, key_rows) * score_scale
    weights = jnp.exp(scores) * allowed
    row_total = lax.optimization_barrier(jnp.sum(weights, axis=-1, keepdims=True))
    softmax_low = (weights / row_total).astype(jnp.bfloat16)
    output = jnp.einsum('whqk,wkhe->wqhe', softmax_low.astype(jnp.float32), value_rows)
    return (output.astype(jnp.bfloat16), jnp.log(row_total))

def attend_back(windows, log_total, grad_windows, allowed):
    score_scale = HEAD_DIM ** (-0.5)
    query_rows = windows[:, :, 0].astype(jnp.float32)
    key_rows = windows[:, :, 1].astype(jnp.float32)
    value_rows = windows[:, :, 2].astype(jnp.float32)
    grad_rows = grad_windows.astype(jnp.float32)
    scores = jnp.einsum('wqhe,wkhe->whqk', query_rows, key_rows) * score_scale
    softmax_full = jnp.exp(scores - log_total) * allowed
    softmax_low = softmax_full.astype(jnp.bfloat16).astype(jnp.float32)
    grad_value = jnp.einsum('whqk,wqhe->wkhe', softmax_low, grad_rows)
    grad_probs = jnp.einsum('wqhe,wkhe->whqk', grad_rows, value_rows)
    centre = lax.optimization_barrier(jnp.sum(softmax_full * grad_probs, axis=-1, keepdims=True))
    grad_scores = (softmax_full * (grad_probs - centre) * score_scale).astype(jnp.bfloat16).astype(jnp.float32)
    grad_query = jnp.einsum('whqk,wkhe->wqhe', grad_scores, key_rows)
    grad_key = jnp.einsum('whqk,wqhe->wkhe', grad_scores, query_rows)
    return (grad_query, grad_key, grad_value)

def layer_forward(inputs, w_qkv, w_proj, w_fc1, w_fc2, gains, biases, shifted):
    tokens, images, width = inputs.shape
    heads = width // HEAD_DIM
    head_group = width // N_TENSOR
    unit_group = FF // N_TENSOR
    residual = inputs.astype(jnp.float32)
    normed, normal_a, inverse_a = layer_norm(residual, gains[0], biases[0])
    attn_input = normed.astype(jnp.bfloat16)
    qkv_bias = jnp.stack([biases[1], jnp.zeros_like(biases[1]), biases[2]]).astype(jnp.float32)
    projected = jnp.einsum('tbd,dch->tbch', attn_input.astype(jnp.float32), w_qkv.astype(jnp.float32)) + qkv_bias
    windows = to_windows(projected.astype(jnp.bfloat16).reshape(tokens, images, 3 * width), shifted)
    windows = windows.reshape(-1, WIN * WIN, 3, heads, HEAD_DIM)
    allowed = window_keep(shifted, images)
    attended, log_total = attend(windows, allowed)
    attn_tokens = from_windows(attended.reshape(-1, WIN * WIN, width), images, shifted)

    def attn_term(index):
        lower, upper = (index * head_group, (index + 1) * head_group)
        return jnp.einsum('tbh,hd->tbd', attn_tokens[:, :, lower:upper].astype(jnp.float32), w_proj[lower:upper].astype(jnp.float32))
    middle = residual + group_sum(attn_term, N_TENSOR) + biases[3]
    normed_b, normal_b, inverse_b = layer_norm(middle, gains[1], biases[4])
    mlp_input = normed_b.astype(jnp.bfloat16)
    fc_bias = biases[6:].reshape(-1).astype(jnp.float32)
    pre_act = jnp.einsum('tbd,df->tbf', mlp_input.astype(jnp.float32), w_fc1.astype(jnp.float32)) + fc_bias
    hidden = exact_gelu(pre_act).astype(jnp.bfloat16)

    def mlp_term(index):
        lower, upper = (index * unit_group, (index + 1) * unit_group)
        return jnp.einsum('tbf,fd->tbd', hidden[:, :, lower:upper].astype(jnp.float32), w_fc2[lower:upper].astype(jnp.float32))
    output = (middle + group_sum(mlp_term, N_TENSOR) + biases[5]).astype(jnp.bfloat16)
    saved = (normal_a, inverse_a, attn_input, windows, log_total, attn_tokens, normal_b, inverse_b, mlp_input, pre_act, hidden)
    return (output, saved)

def layer_backward(grad, saved, w_qkv, w_proj, w_fc1, w_fc2, gains, biases, shifted):
    normal_a, inverse_a, attn_input, windows, log_total, attn_tokens, normal_b, inverse_b, mlp_input, pre_act, hidden = saved
    tokens, images, width = grad.shape
    heads = width // HEAD_DIM
    head_group = width // N_TENSOR
    unit_group = FF // N_TENSOR
    grad_low = round_trip(grad)
    grad_fc2 = jnp.einsum('tbf,tbd->fd', hidden.astype(jnp.float32), grad_low)
    grad_hidden = jnp.einsum('tbd,fd->tbf', grad_low, w_fc2.astype(jnp.float32))
    grad_pre = jax.vjp(exact_gelu, pre_act)[1](grad_hidden)[0]
    grad_pre_low = round_trip(grad_pre)
    grad_fc1 = jnp.einsum('tbd,tbf->df', mlp_input.astype(jnp.float32), grad_pre_low)

    def back_term(index):
        lower, upper = (index * unit_group, (index + 1) * unit_group)
        return jnp.einsum('tbf,df->tbd', grad_pre_low[:, :, lower:upper], w_fc1[:, lower:upper].astype(jnp.float32))
    grad_mlp_in = group_sum(back_term, N_TENSOR)
    grad_mid = grad + norm_back(grad_mlp_in, normal_b, inverse_b, gains[1])
    grad_mid_low = round_trip(grad_mid)
    grad_proj = jnp.einsum('tbh,tbd->hd', attn_tokens.astype(jnp.float32), grad_mid_low)
    grad_attn = jnp.einsum('tbd,hd->tbh', grad_mid_low, w_proj.astype(jnp.float32)).astype(jnp.bfloat16)
    grad_windows = to_windows(grad_attn, shifted).reshape(-1, WIN * WIN, heads, HEAD_DIM)
    allowed = window_keep(shifted, images)
    grad_query, grad_key, grad_value = attend_back(windows, log_total, grad_windows, allowed)
    stacked = jnp.stack([grad_query, grad_key, grad_value], axis=2).astype(jnp.bfloat16)
    grad_qkv_low = from_windows(stacked.reshape(-1, WIN * WIN, 3 * width), images, shifted)
    grad_qkv_low = grad_qkv_low.reshape(tokens, images, 3, width).astype(jnp.float32)
    grad_qkv = jnp.einsum('tbd,tbch->dch', attn_input.astype(jnp.float32), grad_qkv_low)

    def qkv_term(index):
        lower, upper = (index * head_group, (index + 1) * head_group)
        return jnp.einsum('tbch,dch->tbd', grad_qkv_low[:, :, :, lower:upper], w_qkv[:, :, lower:upper].astype(jnp.float32))
    grad_attn_in = group_sum(qkv_term, N_TENSOR)
    grad_inputs = grad_mid + norm_back(grad_attn_in, normal_a, inverse_a, gains[0])
    gain_grads = jnp.stack([lax.optimization_barrier(jnp.sum(grad_attn_in * normal_a, axis=(0, 1))), lax.optimization_barrier(jnp.sum(grad_mlp_in * normal_b, axis=(0, 1)))])
    bias_rows = jnp.stack([lax.optimization_barrier(jnp.sum(grad_attn_in, axis=(0, 1))), lax.optimization_barrier(jnp.sum(grad_query, axis=(0, 1))).reshape(width), lax.optimization_barrier(jnp.sum(grad_value, axis=(0, 1))).reshape(width), lax.optimization_barrier(jnp.sum(grad_mid, axis=(0, 1))), lax.optimization_barrier(jnp.sum(grad_mlp_in, axis=(0, 1))), lax.optimization_barrier(jnp.sum(grad, axis=(0, 1)))])
    bias_grads = jnp.concatenate([bias_rows, lax.optimization_barrier(jnp.sum(grad_pre, axis=(0, 1))).reshape(-1, width)], axis=0)
    return (grad_inputs, (grad_qkv, grad_proj, grad_fc1, grad_fc2, gain_grads, bias_grads))

def reference(boundary, live, w_qkv, w_proj, w_fc1, w_fc2, gains, biases):
    layers = []
    for layer in range(2):
        layers.append((w_qkv[layer], w_proj[layer], w_fc1[layer], w_fc2[layer], gains[layer], biases[layer]))
    totals = [None, None]
    outputs = []
    grads_in = []
    for micro_index in range(MICRO):
        keep = (jnp.arange(SLOTS)[None, :] < live[micro_index][:, None]).reshape(IMAGES).astype(jnp.float32)
        first_out, first_saved = layer_forward(boundary[0, micro_index], *layers[0], False)
        second_out, second_saved = layer_forward(first_out, *layers[1], True)
        outputs.append(second_out.astype(jnp.float32) * keep[None, :, None])
        cotangent = boundary[1, micro_index].astype(jnp.float32) * keep[None, :, None]
        cross, second_grads = layer_backward(cotangent, second_saved, *layers[1], True)
        grad_inputs, first_grads = layer_backward(round_trip(cross), first_saved, *layers[0], False)
        grads_in.append(grad_inputs)
        for layer, terms in ((0, first_grads), (1, second_grads)):
            if totals[layer] is None:
                totals[layer] = terms
            else:
                totals[layer] = tuple((old + new for old, new in zip(totals[layer], terms)))
    results = jnp.stack([jnp.stack(grads_in), jnp.stack(outputs)])
    stacked = [jnp.stack([totals[0][index], totals[1][index]]) for index in range(6)]
    return (results, stacked[0], stacked[1], stacked[2], stacked[3], stacked[4], stacked[5])
```

```python
import functools

import jax
import jax.numpy as jnp
import numpy as np
from jax import lax
from jax.experimental import pallas as pl
from jax.experimental.pallas import tpu as pltpu
from jax.sharding import PartitionSpec as P

HEAD_DIM = 32
GRID = 14
WIN = 7
SHIFT = 3
EPSILON = 1e-05
TOK = GRID * GRID
D = 512
PAD = 64
IMG = 4 * PAD
GROUP = 8
SCALE = HEAD_DIM ** (-0.5)
F32 = jnp.float32
BF16 = jnp.bfloat16
LIMIT = 60 * 1024 * 1024

ANY = pl.BlockSpec(memory_space=pl.ANY)
VM = pl.BlockSpec(memory_space=pltpu.VMEM)
SM = pl.BlockSpec(memory_space=pltpu.SMEM)


def token_of(shifted):
    rows = -np.ones((IMG,), np.int64)
    for window in range(4):
        for r in range(WIN * WIN):
            row = (window // 2) * WIN + r // WIN
            col = (window % 2) * WIN + r % WIN
            if shifted:
                row, col = (row + SHIFT) % GRID, (col + SHIFT) % GRID
            rows[window * PAD + r] = row * GRID + col
    return rows


def one_hot(rows):
    return (rows[:, None] == np.arange(TOK)[None, :]).astype(np.float32)


def dot(a, b, ca=1, cb=0):
    return lax.dot_general(a, b, (((ca,), (cb,)), ((), ())), preferred_element_type=F32)


def normalize(values):
    centred = values - jnp.mean(values, axis=-1, keepdims=True)
    inverse = lax.rsqrt(jnp.mean(centred * centred, axis=-1, keepdims=True) + EPSILON)
    return centred * inverse, inverse


def norm_back(grad, normal, inverse, gain):
    scaled = grad * gain
    return inverse * (
        scaled
        - jnp.mean(scaled, axis=-1, keepdims=True)
        - normal * jnp.mean(scaled * normal, axis=-1, keepdims=True)
    )


def iota(shape, dim):
    return lax.broadcasted_iota(jnp.int32, shape, dim)


def shr(values, by):
    return lax.shift_right_logical(values, jnp.int32(by))


def head_mask():
    shape = (GROUP * PAD, GROUP * HEAD_DIM)
    return jnp.where(shr(iota(shape, 0), 6) == shr(iota(shape, 1), 5), 1.0, 0.0).astype(BF16)


def block_ones():
    shape = (GROUP * PAD, GROUP * PAD)
    return jnp.where(shr(iota(shape, 0), 6) == shr(iota(shape, 1), 6), 1.0, 0.0).astype(BF16)


def head_ones():
    shape = (GROUP * HEAD_DIM, GROUP * PAD)
    return jnp.where(shr(iota(shape, 0), 5) == shr(iota(shape, 1), 6), 1.0, 0.0).astype(BF16)


def allowed_pairs(window, shifted):
    shape = (PAD, GROUP * PAD)
    query, key = iota(shape, 0), iota(shape, 1) & (PAD - 1)
    allowed = key < WIN * WIN
    if shifted:
        query_row, key_row = shr(query * 37, 8), shr(key * 37, 8)
        query_col, key_col = query - WIN * query_row, key - WIN * key_row
        edge = WIN - SHIFT
        rows = (query_row >= edge) == (key_row >= edge)
        cols = (query_col >= edge) == (key_col >= edge)
        if window // 2 == 1:
            allowed = allowed & rows
        if window % 2 == 1:
            allowed = allowed & cols
    return jnp.where(allowed, 1.0, 0.0).astype(F32)


def spread(rows, mask):
    return jnp.concatenate([rows] * GROUP, axis=0) * mask


def fold(full, mask):
    full = full * mask
    total = full[0:PAD]
    for head in range(1, GROUP):
        total = total + full[head * PAD : (head + 1) * PAD]
    return total


def load_attn_weights(layer, gathered, w_qkv, w_proj, sem):
    copies = []
    height = gathered.shape[1]
    parts = D // height
    for j in range(parts):
        for t in range(4):
            block = gathered.at[(layer * parts + j) * 4 + t]
            rows = pl.ds(j * height, height)
            for c in range(3):
                copies.append((block.at[:, pl.ds(c * 128, 128)], w_qkv.at[rows, pl.ds(c * D + t * 128, 128)]))
            copies.append((block.at[:, pl.ds(384, 128)], w_proj.at[rows, pl.ds(t * 128, 128)]))
    return [pltpu.make_async_copy(src, dst, sem) for src, dst in copies]


def load_mlp_weights(layer, gathered, w_fc1, w_fc2, sem):
    copies = []
    height = gathered.shape[1] // 2
    parts = D // height
    for j in range(parts):
        for t in range(4):
            block = gathered.at[(layer * parts + j) * 4 + t]
            rows, cols = pl.ds(j * height, height), pl.ds(t * D, D)
            copies.append((block.at[pl.ds(0, height)], w_fc1.at[rows, cols]))
            copies.append((block.at[pl.ds(height, height)], w_fc2.at[rows, cols]))
    return [pltpu.make_async_copy(src, dst, sem) for src, dst in copies]


def each(count, body):
    def step(index, carry):
        body(index)
        return carry

    lax.fori_loop(0, count, step, 0)


def image_rows(index):
    return pl.ds(pl.multiple_of(index * IMG, IMG), IMG)


def attn_forward_kernel(
    layer, images, source, perm, vec, gathered,
    x_out, a_out, qkv_out, p_out, attn_out, mid_out,
    w_qkv, w_proj, mask, ones, pairs, sem,
):
    copies = load_attn_weights(layer, gathered, w_qkv, w_proj, sem)
    for copy in copies:
        copy.start()
    mask[...] = head_mask()
    ones[...] = block_ones()
    for window in range(4):
        pairs[window] = allowed_pairs(window, layer == 1)
    for copy in copies:
        copy.wait()
    gain, offset = vec[0:1], vec[2:3]
    query_bias, value_bias, out_bias = vec[3:4], vec[4:5], vec[5:6]

    def one_image(i):
        rows = image_rows(i)
        if layer == 0:
            x = dot(perm[0], source[0, i])
            for t in range(1, 4):
                x = x + dot(perm[t], source[t, i])
        else:
            x = dot(perm[...], source[rows])
        x_out[rows] = x.astype(BF16)
        normal, _ = normalize(x)
        a = (normal * gain + offset).astype(BF16)
        a_out[rows] = a
        qkv_out[rows, 0:D] = (dot(a, w_qkv[:, 0:D]) + query_bias).astype(BF16)
        qkv_out[rows, D : 2 * D] = dot(a, w_qkv[:, D : 2 * D]).astype(BF16)
        qkv_out[rows, 2 * D : 3 * D] = (dot(a, w_qkv[:, 2 * D : 3 * D]) + value_bias).astype(BF16)

        def one_window(w):
            own = pl.ds(pl.multiple_of(i * IMG + w * PAD, PAD), PAD)
            for g in range(2):
                low, high = g * 256, (g + 1) * 256
                q = qkv_out[own, low:high]
                k = spread(qkv_out[own, D + low : D + high], mask[...])
                v = spread(qkv_out[own, 2 * D + low : 2 * D + high], mask[...])
                weights = jnp.exp(dot(q, k, 1, 1) * SCALE) * pairs[w]
                total = dot(weights.astype(BF16), ones[...])
                probs = (weights / total).astype(BF16)
                p_out[i * 4 + w, g] = probs
                attn_out[own, low:high] = dot(probs, v).astype(BF16)

        each(4, one_window)
        mid_out[rows] = x + dot(attn_out[rows], w_proj[...], 1, 1) + out_bias

    each(images, one_image)


def mlp_forward_kernel(
    layer, images, keep, mid, perm, vec, gathered,
    m_out, hidden_out, slope_out, final_out,
    w_fc1, w_fc2, acc, sem,
):
    copies = load_mlp_weights(layer, gathered, w_fc1, w_fc2, sem)
    for copy in copies:
        copy.start()
    for copy in copies:
        copy.wait()
    gain, offset, last_bias = vec[1:2], vec[6:7], vec[7:8]

    def one_image(i):
        rows = image_rows(i)
        normal, _ = normalize(mid[rows])
        m_out[rows] = (normal * gain + offset).astype(BF16)
        acc[...] = mid[rows] + last_bias

        def one_chunk(f):
            cols = pl.ds(pl.multiple_of(f * D, D), D)
            pre = dot(m_out[rows], w_fc1[:, cols]) + vec[pl.ds(8 + f, 1)]
            cdf = 0.5 + 0.5 * lax.erf(pre * np.float32(np.sqrt(0.5)))
            density = jnp.exp(-0.5 * pre * pre) * np.float32(1.0 / np.sqrt(2 * np.pi))
            hidden = (pre * cdf).astype(BF16)
            hidden_out[rows, cols] = hidden
            slope_out[rows, cols] = (cdf + pre * density).astype(BF16)
            acc[...] += dot(hidden, w_fc2[:, cols], 1, 1)

        each(4, one_chunk)
        out = acc[...].astype(BF16)
        if layer == 0:
            final_out[rows] = out
        else:
            for t in range(4):
                final_out[t, i] = (dot(perm[t], out) * keep[i]).astype(BF16)

    each(images, one_image)


def mlp_backward_kernel(
    layer, images, keep, source, perm, mid, m_in, hidden, slope, vec, gathered,
    mid_grad, block_out, sums,
    w_fc1, w_fc2, gz, pre_low, acc, sem,
):
    copies = load_mlp_weights(layer, gathered, w_fc1, w_fc2, sem)
    for copy in copies:
        copy.start()
    sums[...] = jnp.zeros_like(sums)
    for copy in copies:
        copy.wait()
    gain = vec[1:2]

    def one_image(i):
        rows = image_rows(i)
        if layer == 1:
            g = dot(perm[0], source[0, i])
            for t in range(1, 4):
                g = g + dot(perm[t], source[t, i])
            g = g * keep[i]
        else:
            g = dot(perm[...], source[rows])
        gz[rows] = g.astype(BF16)
        acc[...] = jnp.zeros_like(acc)

        def one_chunk(f):
            cols = pl.ds(pl.multiple_of(f * D, D), D)
            grad_pre = dot(gz[rows], w_fc2[:, cols]) * slope[rows, cols].astype(F32)
            sums[pl.ds(8 + f, 1)] += jnp.sum(grad_pre, axis=0, keepdims=True)
            low = grad_pre.astype(BF16)
            pre_low[rows, cols] = low
            acc[...] += dot(low, w_fc1[:, cols], 1, 1)

        each(4, one_chunk)
        grad_in = acc[...]
        normal, inverse = normalize(mid[rows])
        g = gz[rows].astype(F32)
        grad_mid = g + norm_back(grad_in, normal, inverse, gain)
        mid_grad[rows] = grad_mid
        sums[1:2] += jnp.sum(grad_in * normal, axis=0, keepdims=True)
        sums[6:7] += jnp.sum(grad_in, axis=0, keepdims=True)
        sums[7:8] += jnp.sum(g, axis=0, keepdims=True)
        sums[5:6] += jnp.sum(grad_mid, axis=0, keepdims=True)

    each(images, one_image)

    def one_block(f):
        cols = pl.ds(pl.multiple_of(f * D, D), D)
        first = dot(m_in[...], pre_low[:, cols], 0, 0).astype(BF16)
        second = dot(gz[...], hidden[:, cols], 0, 0).astype(BF16)
        height = block_out.shape[1] // 2
        for j in range(D // height):
            block_out[j * 4 + f, 0:height] = first[j * height : (j + 1) * height]
            block_out[j * 4 + f, height : 2 * height] = second[j * height : (j + 1) * height]

    each(4, one_block)


def attn_backward_kernel(
    layer, images, mid_grad, x_in, a_in, qkv, p_in, attn, perm, vec, gathered,
    final_out, block_out, sums,
    w_qkv, w_proj, mask, spread_ones, gy, grad_attn, grad_qkv, sem,
):
    copies = load_attn_weights(layer, gathered, w_qkv, w_proj, sem)
    for copy in copies:
        copy.start()
    mask[...] = head_mask()
    spread_ones[...] = head_ones()
    sums[...] = jnp.zeros_like(sums)
    for copy in copies:
        copy.wait()
    gain = vec[0:1]

    def one_image(i):
        rows = image_rows(i)
        gy[rows] = mid_grad[rows].astype(BF16)
        grad_attn[...] = dot(gy[rows], w_proj[...]).astype(BF16)

        def one_window(w):
            own = pl.ds(pl.multiple_of(i * IMG + w * PAD, PAD), PAD)
            inner = pl.ds(pl.multiple_of(w * PAD, PAD), PAD)
            for g in range(2):
                low, high = g * 256, (g + 1) * 256
                q = qkv[own, low:high]
                k = spread(qkv[own, D + low : D + high], mask[...])
                v = spread(qkv[own, 2 * D + low : 2 * D + high], mask[...])
                out_grad = grad_attn[inner, low:high]
                probs = p_in[i * 4 + w, g]
                weighted = out_grad.astype(F32) * attn[own, low:high].astype(F32)
                centre = dot(weighted.astype(BF16), spread_ones[...])
                probs_grad = dot(out_grad, v, 1, 1)
                scores_grad = (probs.astype(F32) * (probs_grad - centre) * SCALE).astype(BF16)
                grad_query = dot(scores_grad, k)
                keep_mask = mask[...].astype(F32)
                grad_key = fold(dot(scores_grad, q, 0, 0), keep_mask)
                grad_value = fold(dot(probs, out_grad, 0, 0), keep_mask)
                sums[3:4, low:high] += jnp.sum(grad_query, axis=0, keepdims=True)
                sums[4:5, low:high] += jnp.sum(grad_value, axis=0, keepdims=True)
                grad_qkv[own, low:high] = grad_query.astype(BF16)
                grad_qkv[own, D + low : D + high] = grad_key.astype(BF16)
                grad_qkv[own, 2 * D + low : 2 * D + high] = grad_value.astype(BF16)

        each(4, one_window)
        grad_in = dot(grad_qkv[rows], w_qkv[...], 1, 1)
        normal, inverse = normalize(x_in[rows].astype(F32))
        grad_x = (mid_grad[rows] + norm_back(grad_in, normal, inverse, gain)).astype(BF16)
        sums[0:1] += jnp.sum(grad_in * normal, axis=0, keepdims=True)
        sums[2:3] += jnp.sum(grad_in, axis=0, keepdims=True)
        if layer == 1:
            final_out[rows] = grad_x
        else:
            for t in range(4):
                final_out[t, i] = dot(perm[t], grad_x).astype(BF16)

    each(images, one_image)
    height = block_out.shape[1]
    for c in range(4):
        if c < 3:
            full = dot(a_in[...], grad_qkv[:, c * D : (c + 1) * D], 0, 0).astype(BF16)
        else:
            full = dot(gy[...], attn[...], 0, 0).astype(BF16)
        for j in range(D // height):
            for t in range(4):
                block_out[j * 4 + t, :, c * 128 : (c + 1) * 128] = full[
                    j * height : (j + 1) * height, t * 128 : (t + 1) * 128
                ]


def shape(dims, dtype=BF16):
    return jax.ShapeDtypeStruct(dims, dtype)


def block_shape(gathered):
    return shape((gathered.shape[0] // 2,) + gathered.shape[1:])


def call(kernel, name, in_specs, outs, scratch, flops, moved):
    return pl.pallas_call(
        kernel,
        name=name,
        in_specs=in_specs,
        out_specs=[VM] * len(outs),
        out_shape=outs,
        scratch_shapes=scratch,
        compiler_params=pltpu.CompilerParams(vmem_limit_bytes=LIMIT),
        cost_estimate=pl.CostEstimate(flops=flops, bytes_accessed=moved, transcendentals=0),
    )


def attn_forward(layer, images, source, perm, vec, gathered):
    rows = images * IMG
    return call(
        functools.partial(attn_forward_kernel, layer, images),
        f"attn_forward_{layer}",
        [VM, VM, VM, ANY],
        [
            shape((rows, D)), shape((rows, D)), shape((rows, 3 * D)),
            shape((images * 4, 2, PAD, GROUP * PAD)), shape((rows, D)), shape((rows, D), F32),
        ],
        [
            pltpu.VMEM((D, 3 * D), BF16), pltpu.VMEM((D, D), BF16),
            pltpu.VMEM((GROUP * PAD, 256), BF16), pltpu.VMEM((GROUP * PAD, GROUP * PAD), BF16),
            pltpu.VMEM((4, PAD, GROUP * PAD), F32), pltpu.SemaphoreType.DMA,
        ],
        2 * rows * D * 4 * D * 3, 12 << 20,
    )(source, perm, vec, gathered)


def mlp_forward(layer, images, keep, mid, perm, vec, gathered):
    rows = images * IMG
    final = shape((rows, D)) if layer == 0 else shape((4, images, TOK // 4, D))
    return call(
        functools.partial(mlp_forward_kernel, layer, images),
        f"mlp_forward_{layer}",
        [SM, VM, VM, VM, ANY],
        [shape((rows, D)), shape((rows, 4 * D)), shape((rows, 4 * D)), final],
        [
            pltpu.VMEM((D, 4 * D), BF16), pltpu.VMEM((D, 4 * D), BF16),
            pltpu.VMEM((IMG, D), F32), pltpu.SemaphoreType.DMA,
        ],
        2 * rows * D * 8 * D * 3, 14 << 20,
    )(keep, mid, perm, vec, gathered)


def mlp_backward(layer, images, keep, source, perm, mid, m_in, hidden, slope, vec, gathered):
    rows = images * IMG
    return call(
        functools.partial(mlp_backward_kernel, layer, images),
        f"mlp_backward_{layer}",
        [SM] + [VM] * 7 + [ANY],
        [shape((rows, D), F32), block_shape(gathered), shape((16, D), F32)],
        [
            pltpu.VMEM((D, 4 * D), BF16), pltpu.VMEM((D, 4 * D), BF16),
            pltpu.VMEM((rows, D), BF16), pltpu.VMEM((rows, 4 * D), BF16),
            pltpu.VMEM((IMG, D), F32), pltpu.SemaphoreType.DMA,
        ],
        2 * rows * D * 16 * D * 2, 20 << 20,
    )(keep, source, perm, mid, m_in, hidden, slope, vec, gathered)


def attn_backward(layer, images, mid_grad, x_in, a_in, qkv, p_in, attn, perm, vec, gathered):
    rows = images * IMG
    final = shape((rows, D)) if layer == 1 else shape((4, images, TOK // 4, D))
    return call(
        functools.partial(attn_backward_kernel, layer, images),
        f"attn_backward_{layer}",
        [VM] * 8 + [ANY],
        [final, block_shape(gathered), shape((16, D), F32)],
        [
            pltpu.VMEM((D, 3 * D), BF16), pltpu.VMEM((D, D), BF16),
            pltpu.VMEM((GROUP * PAD, 256), BF16), pltpu.VMEM((256, GROUP * PAD), BF16),
            pltpu.VMEM((rows, D), BF16), pltpu.VMEM((IMG, D), BF16), pltpu.VMEM((rows, 3 * D), BF16),
            pltpu.SemaphoreType.DMA,
        ],
        2 * rows * D * 8 * D * 4, 16 << 20,
    )(mid_grad, x_in, a_in, qkv, p_in, attn, perm, vec, gathered)


def permutations():
    plain, rolled = one_hot(token_of(False)), one_hot(token_of(True))
    quarter = TOK // 4

    def pieces(matrix):
        return jnp.asarray(matrix.reshape(IMG, 4, quarter).transpose(1, 0, 2), BF16)

    def back(matrix):
        return jnp.asarray(matrix.reshape(IMG, 4, quarter).transpose(1, 2, 0), BF16)

    step = rolled @ plain.T
    return pieces(plain), back(plain), pieces(rolled), back(rolled), jnp.asarray(step, BF16), jnp.asarray(step.T, BF16)


def compute(x_in, cot_in, keep, vec, attn_w, mlp_w):
    images = x_in.shape[1]
    plain, plain_back, rolled, rolled_back, step, step_back = permutations()
    x0, a0, qkv0, p0, attn0, mid0 = attn_forward(0, images, x_in, plain, vec[0], attn_w)
    m0, hid0, slope0, h = mlp_forward(0, images, keep, mid0, step, vec[0], mlp_w)
    x1, a1, qkv1, p1, attn1, mid1 = attn_forward(1, images, h, step, vec[1], attn_w)
    m1, hid1, slope1, out = mlp_forward(1, images, keep, mid1, rolled_back, vec[1], mlp_w)
    gmid1, gm1, s_m1 = mlp_backward(1, images, keep, cot_in, rolled, mid1, m1, hid1, slope1, vec[1], mlp_w)
    cross, ga1, s_a1 = attn_backward(1, images, gmid1, x1, a1, qkv1, p1, attn1, step, vec[1], attn_w)
    gmid0, gm0, s_m0 = mlp_backward(0, images, keep, cross, step_back, mid0, m0, hid0, slope0, vec[0], mlp_w)
    grad_x, ga0, s_a0 = attn_backward(0, images, gmid0, x0, a0, qkv0, p0, attn0, plain_back, vec[0], attn_w)
    return out, grad_x, (ga0, ga1), (gm0, gm1), (s_a0 + s_m0, s_a1 + s_m1)


def shards(boundary, live, w_qkv, w_proj, w_fc1, w_fc2, gains, biases):
    everyone = ("section", "dp", "tensor")
    section = lax.axis_index("section")
    tensor = lax.axis_index("tensor")
    micro, quarter, slots = boundary.shape[1:4]
    images = slots // 2
    n_dp = lax.axis_size("dp")
    own = boundary[0].reshape(micro, quarter, 2, images, D).transpose(2, 0, 3, 1, 4)
    own = own.reshape(2 * micro, images, quarter, D)
    taken = lax.all_to_all(own, ("section", "tensor"), 0, 0, tiled=True)
    x_in, cot_in = taken[:micro], taken[micro:]
    mine = lax.dynamic_index_in_dim(live, tensor, 0, keepdims=False)[0]
    keep = (section * images + jnp.arange(images) < mine).astype(F32)

    attn_shard = jnp.concatenate([w_qkv[0].reshape(-1, 384), w_proj[0].T], axis=1)
    mlp_shard = jnp.concatenate([w_fc1[0], w_fc2[0].T], axis=0)
    attn_w = lax.all_gather(attn_shard, everyone, axis=0, tiled=False)
    mlp_w = lax.all_gather(mlp_shard, everyone, axis=0, tiled=False)
    small = jnp.concatenate([gains[0], biases[0], jnp.zeros((4, gains.shape[2]), BF16)], axis=0)
    vec = lax.all_gather(small, ("section", "dp"), axis=0, tiled=False)
    vec = vec.reshape(2, n_dp, 16, -1).transpose(0, 2, 1, 3).reshape(2, 16, D).astype(F32)

    out, grad_x, ga, gm, sums = compute(x_in, cot_in, keep, vec, attn_w, mlp_w)

    ga = lax.psum_scatter(jnp.concatenate(ga, axis=0), everyone, scatter_dimension=0, tiled=True)[0]
    gm = lax.psum_scatter(jnp.concatenate(gm, axis=0), everyone, scatter_dimension=0, tiled=True)[0]
    ga, gm = ga.astype(F32), gm.astype(F32)
    sums = jnp.stack(sums)[:, :12].reshape(2, 12, -1, D // (lax.axis_size("dp") * lax.axis_size("tensor")))
    sums = sums.transpose(0, 2, 1, 3)
    sums = lax.psum_scatter(sums.reshape((-1,) + sums.shape[2:]), everyone, scatter_dimension=0, tiled=True)[0]

    back = lax.all_to_all(
        jnp.concatenate([grad_x, out], axis=0), ("section", "tensor"), 0, 0, tiled=True
    )
    back = back.reshape(2, micro, images, quarter, D).transpose(1, 3, 0, 2, 4)
    results = back.reshape(micro, quarter, slots, D).astype(F32)
    return (
        results[None],
        ga[:, :384].reshape(1, -1, 3, 128),
        ga[:, 384:].T[None],
        gm[None, : D // n_dp],
        gm[D // n_dp :].T[None],
        sums[None, :2],
        sums[None, 2:],
    )


def solution(mesh):
    return jax.shard_map(
        shards,
        mesh=mesh,
        in_specs=(
            P("section", None, "tensor", "dp", None),
            P(None, "dp"),
            P("section", "dp", None, "tensor"),
            P("section", "tensor", "dp"),
            P("section", "dp", "tensor"),
            P("section", "tensor", "dp"),
            P("section", None, "dp"),
            P("section", None, "dp"),
        ),
        out_specs=(
            P("section", None, "tensor", "dp", None),
            P("section", "dp", None, "tensor"),
            P("section", "tensor", "dp"),
            P("section", "dp", "tensor"),
            P("section", "tensor", "dp"),
            P("section", None, ("dp", "tensor")),
            P("section", None, ("dp", "tensor")),
        ),
        check_vma=False,
    )
```
